32 devices in a mesh: cores: 2 (over y), gz: 4 (over z), gy: 2 (over x), col: 2 (over core).
Axes of the slice: x: 2, y: 2, z: 4, core: 2. Of those that a mesh axis runs over, the one named last changes fastest.
Arguments:
- density: bfloat16 [32, 64, 512], P(('cores', 'gz'), 'gy', 'col'), parts along dimension 0, may hold values from -6 to 6
- first_kernel: bfloat16 [27, 8, 1], replicated, may hold values from -1.25 to 1.25
- first_bias: float32 [8], replicated, may hold values from -3 to 3
- second_kernel: bfloat16 [27, 2, 8], replicated, may hold values from -0.625 to 0.625
- second_bias: float32 [2], replicated, may hold values from -3 to 3
- owners: int32 [8, 2, 2, 16, 1], P(('cores', 'gz'), 'gy', 'col'), parts along dimension 0, may hold values from 0 to 3; in each aligned block of 16 rows (0 to 15, 16 to 31, ..., all dimensions but the last counted through in order) at most 8 rows name the same one
- solutes: float32 [8, 2, 2, 32, 2, 4, 4, 128], P(('cores', 'gz'), 'gy', 'col'), parts along dimension 0, may hold values from 0.2 to 2
- biomass: bfloat16 [8, 2, 2, 32, 4, 4, 128], P(('cores', 'gz'), 'gy', 'col'), parts along dimension 0, may hold values from 0.099609375 to 1
Outputs:
- fractions: bfloat16 [2, 32, 64, 512], P(None, ('cores', 'gz'), 'gy', 'col'), parts along dimension 1
- solutes_next: float32 [8, 2, 2, 32, 2, 4, 4, 128], P(('cores', 'gz'), 'gy', 'col'), parts along dimension 0
The draws below stay inside these ranges and needn't reach their ends.
There are 2 independent parts, one for each index of `cores`. The reference program is written for one: setup_inputs(seed, part) draws one part's arguments, and reference() takes and returns one part's arrays. A program takes and returns all parts, laid end to end along the dimension named above; an argument that names none is the same for every part. Nothing has to cross between parts.
Inputs may be any that keep to these rules, and one draw needn't show every extreme that they name: `owners`: among the 16 bricks of one device at most 8 name the same owner, and some device reaches 8.
All inputs are finite; a program needn't handle non-finite values.
Results may differ from the reference program's by a relative error of at most 0.0034.
Values may be sent and summed in bfloat16 or wider, within the bound.
A program may use at most 64 MiB of HBM per device.

```python
import math
import jax
import jax.numpy as jnp
import numpy as np

CH = 8
CZ = 4
CY = 32
CX = 256
BY = 4
BX = 128
STEPS = 4
NB = 16
CAP = 8
SLOTS = 32
NZ = 16
NY = 64
NX = 512
N_GZ = 4
N_GY = 2
N_COL = 2


def block_levels(own_key, dims, pieces, least, largest):
    gain = 1.0
    for position, blocks in pieces:
        steps = jax.random.uniform(jax.random.fold_in(jax.random.fold_in(own_key, 6), position), (blocks,), jnp.float32, least / len(pieces), largest / len(pieces))
        gain = gain * jnp.repeat(jnp.exp(steps), dims[position] // blocks).reshape((-1,) + (1,) * (len(dims) - 1 - position))
    return gain


def routed_block(own_key, own, number, rows, number_of, top, bound, slope):
    sequence = jax.random.permutation(own_key, number_of)
    heavy_load, ordinary = shares(number_of, rows * top, bound, slope, True), shares(number_of, rows * top, bound, slope, False)
    places = jnp.arange(number_of)

    def named(sizes, offset_by):
        used = int((sizes > 0).sum())
        fixed = max(1, used // 4)
        passed = fixed + (places - fixed + offset_by * (used - fixed)) % max(1, number_of - fixed)
        return jnp.zeros((number_of,), jnp.int32).at[sequence[jnp.where(places < fixed, places, passed)]].set(jnp.asarray(sizes, jnp.int32))

    sizes = jnp.where(number % 4 == 0, named(heavy_load, number // 4), named(ordinary, number - number // 4 - 1))
    mixed = jax.random.permutation(jax.random.fold_in(own, 3), number_of)
    donor, taker = mixed[0:number_of // 2 * 2:2], mixed[1:number_of // 2 * 2:2]
    slack = jnp.minimum(sizes[donor] - 1, bound - sizes[taker]) // 2
    slack = jnp.where((donor == sequence[0]) | (taker == sequence[0]) | (sizes[taker] == 0), 0, jnp.maximum(slack, 0))
    passed = jax.random.randint(jax.random.fold_in(own, 4), (number_of // 2,), 0, 1 << 20) % (slack + 1)
    sizes = sizes.at[donor].add(-passed).at[taker].add(passed)
    items = jnp.searchsorted(jnp.cumsum(sizes), jnp.arange(rows * top), side="right").astype(jnp.int32)
    table = items.reshape(top, rows).T
    table = table[jax.random.permutation(jax.random.fold_in(own, 1), rows)]
    offset_by = jax.random.randint(jax.random.fold_in(own, 2), (rows, 1), 0, top)
    return jnp.take_along_axis(table, (jnp.arange(top)[None, :] + offset_by) % top, axis=1)


def shares(count, total, reach, lean, full):
    loads = [(1 << 20) // math.isqrt(grade ** lean) + 1 for grade in range(1, count + 1)]
    largest = reach if full else min(reach, max(-(-total // count), total * loads[0] // sum(loads)))
    least = 1 if total - largest >= count - 1 else 0
    holding, spare = [largest] + [least] * (count - 1), total - largest - least * (count - 1)
    while spare > 0:
        candidates = [i for i in range(1, count) if holding[i] < largest] or [i for i in range(1, count) if holding[i] < reach]
        pool, remaining = sum([loads[i] for i in candidates]), spare
        for i in candidates:
            more = min(reach - holding[i], max(1, remaining * loads[i] // pool), spare)
            holding[i] = holding[i] + more
            spare = spare - more
    return np.array(holding)


def bell_draw(own_key, dims, scale, reach, pieces=(), held_as=jnp.bfloat16):
    loudness = block_levels(own_key, dims, pieces, -0.22, 0.18) if pieces else 1.0
    result = jax.random.normal(own_key, dims, jnp.float32) * scale * loudness
    return jnp.minimum(jnp.maximum(result, -reach), reach).astype(held_as)


def setup_inputs(seed: int = 0, part: int = 0) -> dict:
    keys = jax.random.split(jax.random.key(seed), 9)
    part_keys = jax.random.split(jax.random.fold_in(keys[8], part), 9)
    density = bell_draw(part_keys[0], (NZ, NY, NX), 1.0, 6.0, ((0, 4), (1, 2), (2, 2)))
    first_kernel = bell_draw(keys[1], (27, CH, 1), 27 ** -0.5, 1.25)
    first_bias = bell_draw(keys[2], (CH,), 1.0, 3.0, (), jnp.float32)
    second_kernel = bell_draw(keys[3], (27, 2, CH), (27 * CH // 2) ** -0.5, 0.625)
    second_bias = bell_draw(keys[4], (2,), 1.0, 3.0, (), jnp.float32)
    owners_keys = jax.random.split(jax.random.fold_in(part_keys[5], 1), N_GZ * N_GY * N_COL * NB // NB)
    owners_turns = jax.random.permutation(jax.random.fold_in(part_keys[5], 3), N_GZ * N_GY * N_COL * NB // NB)
    owners = jax.vmap(lambda own, number: routed_block(jax.random.fold_in(part_keys[5], 2), own, number, NB, N_GZ, 1, CAP, 2))(owners_keys, owners_turns).reshape((N_GZ, N_GY, N_COL, NB, 1))
    solutes = jnp.clip(jnp.exp(math.log(2.0) - 2.3025851 * jax.random.uniform(part_keys[6], (N_GZ, N_GY, N_COL, SLOTS, 2, CZ, BY, BX), jnp.float32) ** block_levels(part_keys[6], (N_GZ, N_GY, N_COL, SLOTS, 2, CZ, BY, BX), ((0, 4), (1, 2), (2, 2)), -0.2, 0.2)), 0.2, 2.0)
    biomass = jnp.clip(jnp.exp(math.log(1.0) - 2.306499 * jax.random.uniform(part_keys[7], (N_GZ, N_GY, N_COL, SLOTS, CZ, BY, BX), jnp.float32) ** block_levels(part_keys[7], (N_GZ, N_GY, N_COL, SLOTS, CZ, BY, BX), ((0, 4), (1, 2), (2, 2)), -0.2, 0.2)), 0.099609375, 1.0).astype(jnp.bfloat16)
    return dict(density=density, first_kernel=first_kernel, first_bias=first_bias, second_kernel=second_kernel, second_bias=second_bias, owners=owners, solutes=solutes, biomass=biomass)


def conv_layer(padded, weights, depth, rows, columns):
    total = jnp.zeros((weights.shape[1], depth, rows, columns), jnp.float32)
    for offset in range(27):
        shift_z = offset // 9
        shift_y = (offset // 3) % 3
        shift_x = offset % 3
        window = padded[:, shift_z:shift_z + depth, shift_y:shift_y + rows, shift_x:shift_x + columns]
        total = total + jnp.einsum("oc,czyx->ozyx", weights[offset].astype(jnp.float32), window.astype(jnp.float32))
    return total


def laplace(field):
    padded = jnp.pad(field, [(0, 0)] * (field.ndim - 3) + [(1, 1), (1, 1), (1, 1)], mode="edge")
    centre = padded[..., 1:-1, 1:-1, 1:-1]
    beside_all = padded[..., 2:, 1:-1, 1:-1] + padded[..., :-2, 1:-1, 1:-1]
    beside_all = beside_all + padded[..., 1:-1, 2:, 1:-1] + padded[..., 1:-1, :-2, 1:-1]
    beside_all = beside_all + padded[..., 1:-1, 1:-1, 2:] + padded[..., 1:-1, 1:-1, :-2]
    return beside_all - 6.0 * centre


def advance(state, arrived, biomass):
    pore = arrived[..., 0, :, :, :].astype(jnp.float32)
    organic = arrived[..., 1, :, :, :].astype(jnp.float32)
    mass = biomass.astype(jnp.float32)
    carbon = state[..., 0, :, :, :]
    oxygen = state[..., 1, :, :, :]
    for step in range(STEPS):
        uptake = 0.25 * mass * carbon / (0.5 + jnp.abs(carbon)) * oxygen / (0.3 + jnp.abs(oxygen))
        carbon_new = carbon + 0.12 * pore * laplace(carbon) + 0.3 * organic - uptake
        oxygen_new = oxygen + 0.16 * pore * laplace(oxygen) - uptake
        carbon, oxygen = carbon_new, oxygen_new
    return jnp.stack([carbon, oxygen], axis=-4)


def reference(density, first_kernel, first_bias, second_kernel, second_bias, owners, solutes, biomass):
    padded = jnp.pad(density[None], ((0, 0), (1, 1), (1, 1), (1, 1)))
    first = conv_layer(padded, first_kernel, NZ, NY, NX)
    hidden = jnp.maximum(first + first_bias[:, None, None, None], 0.0).astype(jnp.bfloat16)
    padded = jnp.pad(hidden, ((0, 0), (1, 1), (1, 1), (1, 1)))
    second = conv_layer(padded, second_kernel, NZ, NY, NX)
    fractions = jax.nn.sigmoid(second + second_bias[:, None, None, None]).astype(jnp.bfloat16)
    bricks = fractions.reshape(2, N_GZ, CZ, N_GY, CY // BY, BY, N_COL, CX // BX, BX)
    bricks = bricks.transpose(1, 3, 6, 4, 7, 0, 2, 5, 8).reshape(N_GZ, N_GY, N_COL, NB, 2, CZ, BY, BX)
    target = owners[..., 0].astype(jnp.int32)
    onehot = (target[..., None] == jnp.arange(N_GZ, dtype=jnp.int32)).astype(jnp.int32)
    before = jnp.cumsum(onehot, axis=3) - onehot
    rank = jnp.sum(before * onehot, axis=-1).astype(jnp.int32)
    source = jnp.broadcast_to(jnp.arange(N_GZ, dtype=jnp.int32)[:, None, None, None], target.shape)
    row_index = jnp.broadcast_to(jnp.arange(N_GY, dtype=jnp.int32)[None, :, None, None], target.shape)
    col_index = jnp.broadcast_to(jnp.arange(N_COL, dtype=jnp.int32)[None, None, :, None], target.shape)
    slot_index = source * CAP + rank
    arrived = jnp.zeros((N_GZ, N_GY, N_COL, SLOTS, 2, CZ, BY, BX), jnp.bfloat16)
    arrived = arrived.at[target, row_index, col_index, slot_index].set(bricks)
    solutes_next = advance(solutes, arrived, biomass)
    return fractions, solutes_next
```

```python
import functools
import itertools

import jax
import jax.numpy as jnp
from jax import lax
from jax.experimental import pallas as pl
from jax.experimental.pallas import tpu as pltpu
from jax.sharding import PartitionSpec as P

BY = 4
BX = 128
STEPS = 4
MESH = pl.DeviceIdType.MESH
F32 = jnp.float32
BF16 = jnp.bfloat16
AROUND = [d for d in itertools.product((-1, 0, 1), repeat=3) if d != (0, 0, 0)]
PLACE_Z = {0: (0, 4), 1: (4, 2), -1: (6, 2)}
PLACE_Y = {0: (0, 32), 1: (32, 16), -1: (48, 16)}
PLACE_X = {0: (0, 256), 1: (256, 128), -1: (384, 128)}
TAKE_Z = {0: (0, 4), 1: (0, 2), -1: (2, 2)}
TAKE_Y = {0: (0, 32), 1: (0, 16), -1: (16, 16)}
TAKE_X = {0: (0, 256), 1: (0, 128), -1: (128, 128)}
KR = 48
HR = 34
LANES = 384


def region(ref, tables, offset):
    return ref.at[tuple(pl.ds(*table[o]) for table, o in zip(tables, offset))]


def iota(shape, dim):
    return lax.broadcasted_iota(jnp.int32, shape, dim)


def onehot(condition):
    return jnp.where(condition, 1.0, 0.0).astype(BF16)


def dot(a, b):
    return jnp.dot(a, b, preferred_element_type=F32)


def build_first(w1):
    hidden = w1.shape[1]
    rows, cols = hidden * HR, 9 * KR
    i = iota((rows, 1), 0)
    channel, yi = lax.div(i, HR), lax.rem(i, HR)
    expand = onehot(channel == iota((rows, hidden), 1))
    by_row = lax.dot_general(
        expand, w1, (((1,), (1,)), ((), ())), preferred_element_type=F32
    ).astype(BF16)
    j = iota((1, cols), 1)
    tap, r = lax.div(j, KR), lax.rem(j, KR)
    y = jnp.where(r < 40, r, r - KR)
    tap_offset = lax.div(tap, 3) * 9 + lax.rem(tap, 3)
    total = jnp.zeros((rows, cols), F32)
    for dy in range(3):
        pick = onehot(iota((27, cols), 0) == tap_offset + 3 * dy)
        total = total + jnp.where(y == yi + (dy - 2), dot(by_row, pick), 0.0)
    return total.astype(BF16)


def build_second(w2, first_row, last_row):
    hidden = w2.shape[1]
    rows, cols = 192, hidden * HR
    i = iota((rows, 1), 0)
    group, y = lax.div(i, 32), lax.rem(i, 32)
    j = iota((1, cols), 1)
    yi = lax.rem(j, HR)
    inside = jnp.logical_not(((yi == 0) & first_row) | ((yi == HR - 1) & last_row))
    yi = jnp.where(inside, yi, -100)
    pick = onehot(iota((hidden, cols), 0) == lax.div(j, HR))
    blocks = []
    for dz in range(3):
        total = jnp.zeros((rows, cols), F32)
        for dy in range(3):
            select = onehot(iota((rows, 54), 1) == (9 * dz + 3 * dy) * 2 + group)
            values = dot(dot(select, w2).astype(BF16), pick)
            total = total + jnp.where(yi == y + dy, values, 0.0)
        blocks.append(total.astype(BF16))
    return blocks


def build_placing(owners_ref, slots, capacity):
    count = owners_ref.shape[0]
    target = [owners_ref[b] for b in range(count)]
    j = iota((1, 128), 1)
    brick = ((j & 31) >> 2) * 2 + (j >> 6)
    slot = jnp.zeros((1, 128), jnp.int32)
    for b in range(count):
        rank = jnp.int32(0)
        for other in range(b):
            rank = rank + jnp.where(target[other] == target[b], 1, 0)
        slot = jnp.where(brick == b, target[b] * capacity + rank, slot)
    column = slot * 8 + ((j >> 5) & 1) * 4 + (j & 3)
    i = iota((slots * 8, 1), 0)
    owner = lax.div(i, capacity * 8)
    row = (owner * capacity + lax.rem(i, capacity)) * 8 + lax.rem(lax.div(i, capacity), 8)
    return onehot(row == column)


def diffuse(carbon, oxygen, pore, organic, mass, lane):
    low, high = lane == 0, lane == BX - 1
    pore_c = [0.12 * v for v in pore]
    pore_o = [0.16 * v for v in pore]
    gain = [0.3 * v for v in organic]
    mass = [0.25 * v for v in mass]

    def laplace(field, q):
        z, y = q // 4, q % 4
        v = field[q]
        total = jnp.where(low, v, pltpu.roll(v, 1, 1)) + jnp.where(high, v, pltpu.roll(v, BX - 1, 1))
        near = 2
        for ok, at in ((z > 0, q - 4), (z < 3, q + 4), (y > 0, q - 1), (y < 3, q + 1)):
            if ok:
                total = total + field[at]
                near += 1
        return total - float(near) * v

    for _ in range(STEPS):
        carbon_new, oxygen_new = [], []
        for q in range(16):
            c, o = carbon[q], oxygen[q]
            uptake = mass[q] * c * o / ((0.5 + jnp.abs(c)) * (0.3 + jnp.abs(o)))
            carbon_new.append(c + pore_c[q] * laplace(carbon, q) + gain[q] - uptake)
            oxygen_new.append(o + pore_o[q] * laplace(oxygen, q) - uptake)
        carbon, oxygen = carbon_new, oxygen_new
    return carbon, oxygen


def kernel(
    sizes, capacity,
    density, w1_ref, b1_ref, w2_ref, b2_ref, owners_ref, solutes, biomass,
    fractions, solutes_next,
    tile, first, second, shifted, hidden, frac, out, arrived, state, state_new, mass_in, mass, gathered,
    halo_send, halo_recv, brick_send, brick_recv, local_sem, group_sem,
):
    n, n_gy, n_col = sizes
    slots = n * capacity
    here = (lax.axis_index("gz"), lax.axis_index("gy"), lax.axis_index("col"))
    me = here[0]

    def exists(offset):
        ok = None
        for position, size, o in zip(here, sizes, offset):
            test = None if o == 0 else (position + o >= 0) & (position + o < size)
            ok = test if ok is None else ok if test is None else ok & test
        return ok

    def device(offset):
        return {"gz": here[0] + offset[0], "gy": here[1] + offset[1], "col": here[2] + offset[2]}

    def halo(offset, index, receiver):
        seen = tuple(-o for o in offset) if not receiver else offset
        return pltpu.make_async_remote_copy(
            src_ref=region(density, (TAKE_Z, TAKE_Y, TAKE_X), seen),
            dst_ref=region(tile, (PLACE_Z, PLACE_Y, PLACE_X), seen),
            send_sem=halo_send.at[index],
            recv_sem=halo_recv.at[AROUND.index(seen)],
            device_id=device(offset),
            device_id_type=MESH,
        )

    tile[...] = jnp.zeros_like(tile)
    barrier = pltpu.get_barrier_semaphore()
    expected = jnp.int32(n - 1)
    for offset in AROUND:
        ok = exists(offset)
        expected = expected + jnp.where(ok, 1, 0)

        @pl.when(ok)
        def _():
            pl.semaphore_signal(barrier, inc=1, device_id=device(offset), device_id_type=MESH)

    for j in range(1, n):
        pl.semaphore_signal(
            barrier, inc=1, device_id={"gz": lax.rem(me + j, n)}, device_id_type=MESH
        )
    own = pltpu.make_async_copy(
        density, region(tile, (PLACE_Z, PLACE_Y, PLACE_X), (0, 0, 0)), local_sem.at[0]
    )
    own.start()
    load_state = pltpu.make_async_copy(solutes, state, local_sem.at[1])
    load_mass = pltpu.make_async_copy(biomass, mass_in, local_sem.at[2])
    pl.semaphore_wait(barrier, expected)

    for index, offset in enumerate(AROUND):

        @pl.when(exists(offset))
        def _():
            halo(offset, index, False).start()

    load_state.start()
    load_mass.start()

    first[...] = build_first(w1_ref[...])
    for dz, block in enumerate(build_second(w2_ref[...], here[1] == 0, here[1] == n_gy - 1)):
        second[dz] = block
    placing = build_placing(owners_ref, slots, capacity)
    channel = lax.div(iota((272, 1), 0), HR)
    bias1 = jnp.zeros((272, 1), F32)
    for o in range(8):
        bias1 = jnp.where(channel == o, b1_ref[o], bias1)
    bias2 = jnp.where(iota((64, 1), 0) < 32, b2_ref[0], b2_ref[1])
    lane = iota((1, BX), 1)
    keep = jnp.where(
        ((lane == 0) & (here[2] < n_col - 1)) | ((lane == BX - 1) & (here[2] > 0)), 1.0, 0.0
    )
    load_mass.wait()
    for g in range(slots // 8):
        mass[g] = mass_in[g].astype(F32)

    own.wait()
    for index, offset in enumerate(AROUND):

        @pl.when(exists(offset))
        def _():
            halo(offset, index, True).wait_recv()

    half_row = iota((16, 512), 0) < 8
    half_lane = iota((KR, BX), 1) < 64
    for zz in range(8):
        z = (zz + 6) % 8
        side = jnp.where(half_row, tile[z, 32:48, :].astype(F32), tile[z, 48:64, :].astype(F32))
        whole = jnp.concatenate([tile[z, 0:32, :].astype(F32), side], axis=0)
        edge = jnp.where(half_lane, whole[:, 256:384], whole[:, 384:512])
        whole = jnp.concatenate([whole[:, :256], edge], axis=1)
        base = zz * 3 * KR
        shifted[base : base + KR, :] = pltpu.roll(whole, 1, 1).astype(BF16)
        shifted[base + KR : base + 2 * KR, :] = whole.astype(BF16)
        shifted[base + 2 * KR : base + 3 * KR, :] = pltpu.roll(whole, LANES - 1, 1).astype(BF16)

    def hidden_slice(zi):
        value = dot(first[...], shifted[zi * 3 * KR : (zi + 3) * 3 * KR, :])
        value = jnp.maximum(value + bias1, 0.0)
        hidden[zi, :, 0:256] = value[:, :256].astype(BF16)
        hidden[zi, :, 256:384] = (value[:, 256:] * keep).astype(BF16)

    def brick_copy(j, z):
        to = lax.rem(me + j, n)
        return pltpu.make_async_remote_copy(
            src_ref=out.at[to, z],
            dst_ref=arrived.at[me, z],
            send_sem=brick_send.at[j, z],
            recv_sem=brick_recv.at[j, z],
            device_id={"gz": to},
            device_id_type=MESH,
        )

    hidden_slice(0)

    @pl.when(me == 0)
    def _():
        hidden[0] = jnp.zeros_like(hidden[0])

    hidden_slice(1)
    per = 8 * capacity
    for z in range(4):
        hidden_slice(z + 2)
        if z == 3:

            @pl.when(me == n - 1)
            def _():
                hidden[5] = jnp.zeros_like(hidden[5])

        total = jnp.zeros((192, LANES), F32)
        for dz in range(3):
            total = total + dot(second[dz], hidden[z + dz])
        value = (
            pltpu.roll(total[0:64], 1, 1) + total[64:128] + pltpu.roll(total[128:192], LANES - 1, 1)
        )[:, :256]
        value = (1.0 / (1.0 + jnp.exp(-(value + bias2)))).astype(BF16)
        frac[0, z] = value[:32]
        frac[1, z] = value[32:]
        placed = dot(placing, jnp.concatenate([value[:, :128], value[:, 128:]], axis=0)).astype(BF16)
        for d in range(n):
            out[d, z] = placed[d * per : (d + 1) * per]
        for j in range(1, n):
            brick_copy(j, z).start()
    store_frac = pltpu.make_async_copy(frac, fractions, local_sem.at[3])
    store_frac.start()

    load_state.wait()

    def received(j, z):
        source = lax.rem(me - j + n, n)
        pltpu.make_async_remote_copy(
            src_ref=out.at[source, z],
            dst_ref=arrived.at[source, z],
            send_sem=brick_send.at[j, z],
            recv_sem=brick_recv.at[j, z],
            device_id={"gz": source},
            device_id_type=MESH,
        ).wait_recv()

    def group_copy(g):
        return pltpu.make_async_copy(state_new.at[g], solutes_next.at[g], group_sem.at[g])

    def group(g, pore, organic):
        carbon = [state[g, pl.ds(q, 8, stride=32), :] for q in range(16)]
        oxygen = [state[g, pl.ds(16 + q, 8, stride=32), :] for q in range(16)]
        held = [mass[g, pl.ds(q, 8, stride=16), :] for q in range(16)]
        carbon, oxygen = diffuse(carbon, oxygen, pore, organic, held, iota((8, BX), 1))
        for q in range(16):
            state_new[g, pl.ds(q, 8, stride=32), :] = carbon[q]
            state_new[g, pl.ds(16 + q, 8, stride=32), :] = oxygen[q]
        group_copy(g).start()

    if capacity == 8:
        for j in range(n):
            source = lax.rem(me - j + n, n)
            values = [[None] * 16, [None] * 16]
            for z in range(4):
                if j:
                    received(j, z)
                ref = arrived if j else out
                for o in range(2):
                    for pair in range(2):
                        at = o * 32 + pair * 16
                        both = ref[source, z, at : at + 16, :].astype(F32)
                        values[o][z * 4 + pair * 2] = both[:8]
                        values[o][z * 4 + pair * 2 + 1] = both[8:]
            group(source, *values)
    else:
        for z in range(4):
            arrived[me, z] = out[me, z]
        for j in range(1, n):
            for z in range(4):
                received(j, z)
        for s in range(n):
            for z in range(4):
                block = arrived[s, z].astype(F32)
                for o in range(2):
                    for y in range(4):
                        at = (o * 4 + y) * capacity
                        gathered[o * 16 + z * 4 + y, s * capacity : (s + 1) * capacity, :] = block[
                            at : at + capacity
                        ]

        @pl.loop(0, slots // 8)
        def _(g):
            start = pl.multiple_of(g * 8, 8)
            group(
                g,
                [gathered[q, pl.ds(start, 8), :] for q in range(16)],
                [gathered[16 + q, pl.ds(start, 8), :] for q in range(16)],
            )

    for index, offset in enumerate(AROUND):

        @pl.when(exists(offset))
        def _():
            halo(offset, index, False).wait_send()

    for j in range(1, n):
        for z in range(4):
            brick_copy(j, z).wait_send()
    store_frac.wait()
    for g in range(slots // 8):
        group_copy(g).wait()


def per_device(
    sizes, density, first_kernel, first_bias, second_kernel, second_bias, owners, solutes, biomass
):
    n = sizes[0]
    slots = solutes.shape[3]
    capacity = slots // n
    per = 8 * capacity
    vmem, smem = pl.BlockSpec(memory_space=pltpu.VMEM), pl.BlockSpec(memory_space=pltpu.SMEM)
    anywhere = pl.BlockSpec(memory_space=pl.ANY)
    groups = slots // 8
    fractions, solutes_next = pl.pallas_call(
        functools.partial(kernel, sizes, capacity),
        out_shape=(
            jax.ShapeDtypeStruct((2,) + density.shape, BF16),
            jax.ShapeDtypeStruct((groups, 256, BX), F32),
        ),
        in_specs=[anywhere, vmem, smem, vmem, smem, smem, anywhere, anywhere],
        out_specs=(anywhere, anywhere),
        scratch_shapes=[
            pltpu.VMEM((8, 64, 512), BF16),
            pltpu.VMEM((272, 9 * KR), BF16),
            pltpu.VMEM((3, 192, 272), BF16),
            pltpu.VMEM((8 * 3 * KR, LANES), BF16),
            pltpu.VMEM((6, 272, LANES), BF16),
            pltpu.VMEM((2,) + density.shape, BF16),
            pltpu.VMEM((n, 4, per, BX), BF16),
            pltpu.VMEM((n, 4, per, BX), BF16),
            pltpu.VMEM((groups, 256, BX), F32),
            pltpu.VMEM((groups, 256, BX), F32),
            pltpu.VMEM((groups, 128, BX), BF16),
            pltpu.VMEM((groups, 128, BX), F32),
            pltpu.VMEM((32, slots if capacity != 8 else 8, BX), F32),
            pltpu.SemaphoreType.DMA((26,)),
            pltpu.SemaphoreType.DMA((26,)),
            pltpu.SemaphoreType.DMA((n, 4)),
            pltpu.SemaphoreType.DMA((n, 4)),
            pltpu.SemaphoreType.DMA((4,)),
            pltpu.SemaphoreType.DMA((groups,)),
        ],
        compiler_params=pltpu.CompilerParams(
            collective_id=0, has_side_effects=True, vmem_limit_bytes=32 * 1024 * 1024
        ),
    )(
        density,
        first_kernel.reshape(27, 8),
        first_bias,
        second_kernel.reshape(54, 8),
        second_bias,
        owners.reshape(-1),
        solutes.reshape(groups, 256, BX),
        biomass.reshape(groups, 128, BX),
    )
    return fractions, solutes_next.reshape(solutes.shape)


def solution(mesh):
    sizes = tuple(mesh.shape[axis] for axis in ("gz", "gy", "col"))
    return jax.shard_map(
        functools.partial(per_device, sizes),
        mesh=mesh,
        in_specs=(
            P(("cores", "gz"), "gy", "col"),
            P(),
            P(),
            P(),
            P(),
            P(("cores", "gz"), "gy", "col", None, None),
            P(("cores", "gz"), "gy", "col", None, None, None, None, None),
            P(("cores", "gz"), "gy", "col", None, None, None, None),
        ),
        out_specs=(
            P(None, ("cores", "gz"), "gy", "col"),
            P(("cores", "gz"), "gy", "col", None, None, None, None, None),
        ),
        check_vma=False,
    )
```

```python
import functools
import itertools

import jax
import jax.numpy as jnp
from jax import lax
from jax.experimental import pallas as pl
from jax.experimental.pallas import tpu as pltpu
from jax.sharding import PartitionSpec as P

BY = 4
BX = 128
STEPS = 4
MESH = pl.DeviceIdType.MESH
F32 = jnp.float32
BF16 = jnp.bfloat16
AROUND = [d for d in itertools.product((-1, 0, 1), repeat=3) if d != (0, 0, 0)]
PLACE_Z = {0: (0, 4), 1: (4, 2), -1: (6, 2)}
PLACE_Y = {0: (0, 32), 1: (32, 16), -1: (48, 16)}
PLACE_X = {0: (0, 256), 1: (256, 128), -1: (384, 128)}
TAKE_Z = {0: (0, 4), 1: (0, 2), -1: (2, 2)}
TAKE_Y = {0: (0, 32), 1: (0, 16), -1: (16, 16)}
TAKE_X = {0: (0, 256), 1: (0, 128), -1: (128, 128)}
KR = 48
HR = 34
LANES = 384


def region(ref, tables, offset):
    return ref.at[tuple(pl.ds(*table[o]) for table, o in zip(tables, offset))]


def iota(shape, dim):
    return lax.broadcasted_iota(jnp.int32, shape, dim)


def onehot(condition):
    return jnp.where(condition, 1.0, 0.0).astype(BF16)


def dot(a, b):
    return jnp.dot(a, b, preferred_element_type=F32)


def build_first(w1):
    hidden = w1.shape[0]
    rows, cols = hidden * HR, 9 * KR
    i = iota((rows, 1), 0)
    channel, yi = lax.div(i, HR), lax.rem(i, HR)
    expand = onehot(channel == iota((rows, hidden), 1))
    by_row = dot(expand, w1).astype(BF16)
    j = iota((1, cols), 1)
    tap, r = lax.div(j, KR), lax.rem(j, KR)
    y = jnp.where(r < 40, r, r - KR)
    tap_offset = lax.div(tap, 3) * 9 + lax.rem(tap, 3)
    total = jnp.zeros((rows, cols), F32)
    for dy in range(3):
        pick = onehot(iota((27, cols), 0) == tap_offset + 3 * dy)
        total = total + jnp.where(y == yi + (dy - 2), dot(by_row, pick), 0.0)
    return total.astype(BF16)


def build_second(w2, first_row, last_row):
    hidden = w2.shape[0] // 2
    rows, cols = 192, hidden * HR
    i = iota((rows, 1), 0)
    group, y = lax.div(i, 32), lax.rem(i, 32)
    j = iota((1, cols), 1)
    yi = lax.rem(j, HR)
    inside = jnp.logical_not(((yi == 0) & first_row) | ((yi == HR - 1) & last_row))
    yi = jnp.where(inside, yi, -100)
    pick = onehot(lax.rem(iota((2 * hidden, cols), 0), hidden) == lax.div(j, HR))
    same = lax.rem(group, 2) == lax.div(iota((1, 2 * hidden), 1), hidden)
    blocks = []
    for dz in range(3):
        total = jnp.zeros((rows, cols), F32)
        for dy in range(3):
            select = onehot(iota((rows, 27), 1) == 9 * dz + 3 * dy + lax.div(group, 2))
            values = lax.dot_general(
                select, w2, (((1,), (1,)), ((), ())), preferred_element_type=F32
            )
            values = dot(jnp.where(same, values, 0.0).astype(BF16), pick)
            total = total + jnp.where(yi == y + dy, values, 0.0)
        blocks.append(total.astype(BF16))
    return blocks


def build_placing(owners_ref, slots, capacity):
    count = owners_ref.shape[0]
    target = [owners_ref[b] for b in range(count)]
    j = iota((1, 128), 1)
    brick = ((j & 31) >> 2) * 2 + (j >> 6)
    slot = jnp.zeros((1, 128), jnp.int32)
    for b in range(count):
        rank = jnp.int32(0)
        for other in range(b):
            rank = rank + jnp.where(target[other] == target[b], 1, 0)
        slot = jnp.where(brick == b, target[b] * capacity + rank, slot)
    column = slot * 8 + ((j >> 5) & 1) * 4 + (j & 3)
    i = iota((slots * 8, 1), 0)
    owner = lax.div(i, capacity * 8)
    row = (owner * capacity + lax.rem(i, capacity)) * 8 + lax.rem(lax.div(i, capacity), 8)
    return onehot(row == column)


def diffuse(carbon, oxygen, pore, organic, mass, lane):
    low, high = lane == 0, lane == BX - 1
    pore_c = [0.12 * v for v in pore]
    pore_o = [0.16 * v for v in pore]
    gain = [0.3 * v for v in organic]
    mass = [0.25 * v for v in mass]

    def laplace(field, q):
        z, y = q // 4, q % 4
        v = field[q]
        total = jnp.where(low, v, pltpu.roll(v, 1, 1)) + jnp.where(high, v, pltpu.roll(v, BX - 1, 1))
        near = 2
        for ok, at in ((z > 0, q - 4), (z < 3, q + 4), (y > 0, q - 1), (y < 3, q + 1)):
            if ok:
                total = total + field[at]
                near += 1
        return total - float(near) * v

    for _ in range(STEPS):
        carbon_new, oxygen_new = [], []
        for q in range(16):
            c, o = carbon[q], oxygen[q]
            uptake = mass[q] * c * o / ((0.5 + jnp.abs(c)) * (0.3 + jnp.abs(o)))
            carbon_new.append(c + pore_c[q] * laplace(carbon, q) + gain[q] - uptake)
            oxygen_new.append(o + pore_o[q] * laplace(oxygen, q) - uptake)
        carbon, oxygen = carbon_new, oxygen_new
    return carbon, oxygen


def kernel(
    sizes, capacity,
    density, w1_hbm, b1_hbm, w2_hbm, b2_hbm, owners_hbm, solutes, biomass,
    fractions, solutes_next,
    w1_ref, b1_ref, w2_ref, b2_ref, owners_ref, tile, first, second, shifted, hidden, frac, out, arrived, state, state_new, mass_in, mass, gathered,
    halo_send, halo_recv, brick_send, brick_recv, local_sem, group_sem,
):
    n, n_gy, n_col = sizes
    slots = n * capacity
    here = (lax.axis_index("gz"), lax.axis_index("gy"), lax.axis_index("col"))
    me = here[0]

    def exists(offset):
        ok = None
        for position, size, o in zip(here, sizes, offset):
            test = None if o == 0 else (position + o >= 0) & (position + o < size)
            ok = test if ok is None else ok if test is None else ok & test
        return ok

    def device(offset):
        return {"gz": here[0] + offset[0], "gy": here[1] + offset[1], "col": here[2] + offset[2]}

    def halo(offset, index, receiver):
        seen = tuple(-o for o in offset) if not receiver else offset
        return pltpu.make_async_remote_copy(
            src_ref=region(density, (TAKE_Z, TAKE_Y, TAKE_X), seen),
            dst_ref=region(tile, (PLACE_Z, PLACE_Y, PLACE_X), seen),
            send_sem=halo_send.at[index],
            recv_sem=halo_recv.at[AROUND.index(seen)],
            device_id=device(offset),
            device_id_type=MESH,
        )

    small = [
        pltpu.make_async_copy(source, target, local_sem.at[4 + i])
        for i, (source, target) in enumerate(
            (
                (w1_hbm, w1_ref), (w2_hbm, w2_ref), (b1_hbm, b1_ref), (b2_hbm, b2_ref),
                (owners_hbm, owners_ref),
            )
        )
    ]
    for copy in small:
        copy.start()
    tile[...] = jnp.zeros_like(tile)
    barrier = pltpu.get_barrier_semaphore()
    expected = jnp.int32(n - 1)
    for offset in AROUND:
        ok = exists(offset)
        expected = expected + jnp.where(ok, 1, 0)

        @pl.when(ok)
        def _():
            pl.semaphore_signal(barrier, inc=1, device_id=device(offset), device_id_type=MESH)

    for j in range(1, n):
        pl.semaphore_signal(
            barrier, inc=1, device_id={"gz": lax.rem(me + j, n)}, device_id_type=MESH
        )
    own = pltpu.make_async_copy(
        density, region(tile, (PLACE_Z, PLACE_Y, PLACE_X), (0, 0, 0)), local_sem.at[0]
    )
    own.start()
    load_state = pltpu.make_async_copy(solutes, state, local_sem.at[1])
    load_mass = pltpu.make_async_copy(biomass, mass_in, local_sem.at[2])
    pl.semaphore_wait(barrier, expected)

    for index, offset in enumerate(AROUND):

        @pl.when(exists(offset))
        def _():
            halo(offset, index, False).start()

    load_state.start()
    load_mass.start()

    for copy in small:
        copy.wait()
    first[...] = build_first(w1_ref[...])
    for dz, block in enumerate(build_second(w2_ref[...], here[1] == 0, here[1] == n_gy - 1)):
        second[dz] = block
    placing = build_placing(owners_ref, slots, capacity)
    channel = lax.div(iota((272, 1), 0), HR)
    bias1 = jnp.zeros((272, 1), F32)
    for o in range(8):
        bias1 = jnp.where(channel == o, b1_ref[o], bias1)
    bias2 = jnp.where(iota((64, 1), 0) < 32, b2_ref[0], b2_ref[1])
    lane = iota((1, BX), 1)
    keep = jnp.where(
        ((lane == 0) & (here[2] < n_col - 1)) | ((lane == BX - 1) & (here[2] > 0)), 1.0, 0.0
    )
    load_mass.wait()
    for g in range(slots // 8):
        mass[g] = mass_in[g].astype(F32)

    own.wait()
    for index, offset in enumerate(AROUND):

        @pl.when(exists(offset))
        def _():
            halo(offset, index, True).wait_recv()

    half_row = iota((16, 512), 0) < 8
    half_lane = iota((KR, BX), 1) < 64
    for zz in range(8):
        z = (zz + 6) % 8
        side = jnp.where(half_row, tile[z, 32:48, :].astype(F32), tile[z, 48:64, :].astype(F32))
        whole = jnp.concatenate([tile[z, 0:32, :].astype(F32), side], axis=0)
        edge = jnp.where(half_lane, whole[:, 256:384], whole[:, 384:512])
        whole = jnp.concatenate([whole[:, :256], edge], axis=1)
        base = zz * 3 * KR
        shifted[base : base + KR, :] = pltpu.roll(whole, 1, 1).astype(BF16)
        shifted[base + KR : base + 2 * KR, :] = whole.astype(BF16)
        shifted[base + 2 * KR : base + 3 * KR, :] = pltpu.roll(whole, LANES - 1, 1).astype(BF16)

    def hidden_slice(zi):
        value = dot(first[...], shifted[zi * 3 * KR : (zi + 3) * 3 * KR, :])
        value = jnp.maximum(value + bias1, 0.0)
        hidden[zi, :, 0:256] = value[:, :256].astype(BF16)
        hidden[zi, :, 256:384] = (value[:, 256:] * keep).astype(BF16)

    def brick_copy(j, z):
        to = lax.rem(me + j, n)
        return pltpu.make_async_remote_copy(
            src_ref=out.at[to, z],
            dst_ref=arrived.at[me, z],
            send_sem=brick_send.at[j, z],
            recv_sem=brick_recv.at[j, z],
            device_id={"gz": to},
            device_id_type=MESH,
        )

    hidden_slice(0)

    @pl.when(me == 0)
    def _():
        hidden[0] = jnp.zeros_like(hidden[0])

    hidden_slice(1)
    per = 8 * capacity
    for z in range(4):
        hidden_slice(z + 2)
        if z == 3:

            @pl.when(me == n - 1)
            def _():
                hidden[5] = jnp.zeros_like(hidden[5])

        total = jnp.zeros((192, LANES), F32)
        for dz in range(3):
            total = total + dot(second[dz], hidden[z + dz])
        value = (
            pltpu.roll(total[0:64], 1, 1) + total[64:128] + pltpu.roll(total[128:192], LANES - 1, 1)
        )[:, :256]
        value = (1.0 / (1.0 + jnp.exp(-(value + bias2)))).astype(BF16)
        frac[0, z] = value[:32]
        frac[1, z] = value[32:]
        placed = dot(placing, jnp.concatenate([value[:, :128], value[:, 128:]], axis=0)).astype(BF16)
        for d in range(n):
            out[d, z] = placed[d * per : (d + 1) * per]
        for j in range(1, n):
            brick_copy(j, z).start()
    store_frac = pltpu.make_async_copy(frac, fractions, local_sem.at[3])
    store_frac.start()

    load_state.wait()

    def received(j, z):
        source = lax.rem(me - j + n, n)
        pltpu.make_async_remote_copy(
            src_ref=out.at[source, z],
            dst_ref=arrived.at[source, z],
            send_sem=brick_send.at[j, z],
            recv_sem=brick_recv.at[j, z],
            device_id={"gz": source},
            device_id_type=MESH,
        ).wait_recv()

    def group_copy(g):
        return pltpu.make_async_copy(state_new.at[g], solutes_next.at[g], group_sem.at[g])

    def group(g, pore, organic):
        carbon = [state[g, pl.ds(q, 8, stride=32), :] for q in range(16)]
        oxygen = [state[g, pl.ds(16 + q, 8, stride=32), :] for q in range(16)]
        held = [mass[g, pl.ds(q, 8, stride=16), :] for q in range(16)]
        carbon, oxygen = diffuse(carbon, oxygen, pore, organic, held, iota((8, BX), 1))
        for q in range(16):
            state_new[g, pl.ds(q, 8, stride=32), :] = carbon[q]
            state_new[g, pl.ds(16 + q, 8, stride=32), :] = oxygen[q]
        group_copy(g).start()

    if capacity == 8:
        for j in range(n):
            source = lax.rem(me - j + n, n)
            values = [[None] * 16, [None] * 16]
            for z in range(4):
                if j:
                    received(j, z)
                ref = arrived if j else out
                for o in range(2):
                    for pair in range(2):
                        at = o * 32 + pair * 16
                        both = ref[source, z, at : at + 16, :].astype(F32)
                        values[o][z * 4 + pair * 2] = both[:8]
                        values[o][z * 4 + pair * 2 + 1] = both[8:]
            group(source, *values)
    else:
        for z in range(4):
            arrived[me, z] = out[me, z]
        for j in range(1, n):
            for z in range(4):
                received(j, z)
        for s in range(n):
            for z in range(4):
                block = arrived[s, z].astype(F32)
                for o in range(2):
                    for y in range(4):
                        at = (o * 4 + y) * capacity
                        gathered[o * 16 + z * 4 + y, s * capacity : (s + 1) * capacity, :] = block[
                            at : at + capacity
                        ]

        @pl.loop(0, slots // 8)
        def _(g):
            start = pl.multiple_of(g * 8, 8)
            group(
                g,
                [gathered[q, pl.ds(start, 8), :] for q in range(16)],
                [gathered[16 + q, pl.ds(start, 8), :] for q in range(16)],
            )

    for index, offset in enumerate(AROUND):

        @pl.when(exists(offset))
        def _():
            halo(offset, index, False).wait_send()

    for j in range(1, n):
        for z in range(4):
            brick_copy(j, z).wait_send()
    store_frac.wait()
    for g in range(slots // 8):
        group_copy(g).wait()


def per_device(
    sizes, density, first_kernel, first_bias, second_kernel, second_bias, owners, solutes, biomass
):
    n = sizes[0]
    slots = solutes.shape[3]
    capacity = slots // n
    per = 8 * capacity
    anywhere = pl.BlockSpec(memory_space=pltpu.HBM)
    groups = slots // 8
    fractions, solutes_next = pl.pallas_call(
        functools.partial(kernel, sizes, capacity),
        out_shape=(
            jax.ShapeDtypeStruct((2,) + density.shape, BF16),
            jax.ShapeDtypeStruct((groups, 256, BX), F32),
        ),
        in_specs=[anywhere] * 8,
        out_specs=(anywhere, anywhere),
        scratch_shapes=[
            pltpu.VMEM((8, 27), BF16),
            pltpu.SMEM((8,), F32),
            pltpu.VMEM((16, 27), BF16),
            pltpu.SMEM((2,), F32),
            pltpu.SMEM((16,), jnp.int32),
            pltpu.VMEM((8, 64, 512), BF16),
            pltpu.VMEM((272, 9 * KR), BF16),
            pltpu.VMEM((3, 192, 272), BF16),
            pltpu.VMEM((8 * 3 * KR, LANES), BF16),
            pltpu.VMEM((6, 272, LANES), BF16),
            pltpu.VMEM((2,) + density.shape, BF16),
            pltpu.VMEM((n, 4, per, BX), BF16),
            pltpu.VMEM((n, 4, per, BX), BF16),
            pltpu.VMEM((groups, 256, BX), F32),
            pltpu.VMEM((groups, 256, BX), F32),
            pltpu.VMEM((groups, 128, BX), BF16),
            pltpu.VMEM((groups, 128, BX), F32),
            pltpu.VMEM((32, slots if capacity != 8 else 8, BX), F32),
            pltpu.SemaphoreType.DMA((26,)),
            pltpu.SemaphoreType.DMA((26,)),
            pltpu.SemaphoreType.DMA((n, 4)),
            pltpu.SemaphoreType.DMA((n, 4)),
            pltpu.SemaphoreType.DMA((9,)),
            pltpu.SemaphoreType.DMA((groups,)),
        ],
        compiler_params=pltpu.CompilerParams(
            collective_id=0, has_side_effects=True, vmem_limit_bytes=64 * 1024 * 1024
        ),
    )(
        density,
        first_kernel.transpose(2, 1, 0).reshape(8, 27),
        first_bias,
        second_kernel.transpose(1, 2, 0).reshape(16, 27),
        second_bias,
        owners.reshape(-1),
        solutes.reshape(groups, 256, BX),
        biomass.reshape(groups, 128, BX),
    )
    return fractions, solutes_next.reshape(solutes.shape)


def solution(mesh):
    sizes = tuple(mesh.shape[axis] for axis in ("gz", "gy", "col"))
    return jax.shard_map(
        functools.partial(per_device, sizes),
        mesh=mesh,
        in_specs=(
            P(("cores", "gz"), "gy", "col"),
            P(),
            P(),
            P(),
            P(),
            P(("cores", "gz"), "gy", "col", None, None),
            P(("cores", "gz"), "gy", "col", None, None, None, None, None),
            P(("cores", "gz"), "gy", "col", None, None, None, None),
        ),
        out_specs=(
            P(None, ("cores", "gz"), "gy", "col"),
            P(("cores", "gz"), "gy", "col", None, None, None, None, None),
        ),
        check_vma=False,
    )
```

```python
import functools
import itertools

import jax
import jax.numpy as jnp
from jax import lax
from jax.experimental import pallas as pl
from jax.experimental.pallas import tpu as pltpu
from jax.sharding import PartitionSpec as P

BY = 4
BX = 128
STEPS = 4
MESH = pl.DeviceIdType.MESH
F32 = jnp.float32
BF16 = jnp.bfloat16
AROUND = [d for d in itertools.product((-1, 0, 1), repeat=3) if d != (0, 0, 0)]
PLACE_Z = {0: (0, 4), 1: (4, 2), -1: (6, 2)}
PLACE_Y = {0: (0, 32), 1: (32, 16), -1: (48, 16)}
PLACE_X = {0: (0, 256), 1: (256, 128), -1: (384, 128)}
TAKE_Z = {0: (0, 4), 1: (0, 2), -1: (2, 2)}
TAKE_Y = {0: (0, 32), 1: (0, 16), -1: (16, 16)}
TAKE_X = {0: (0, 256), 1: (0, 128), -1: (128, 128)}
KR = 48
HR = 34
LANES = 384


def region(ref, tables, offset):
    return ref.at[tuple(pl.ds(*table[o]) for table, o in zip(tables, offset))]


def iota(shape, dim):
    return lax.broadcasted_iota(jnp.int32, shape, dim)


def onehot(condition):
    return jnp.where(condition, 1.0, 0.0).astype(BF16)


def dot(a, b):
    return jnp.dot(a, b, preferred_element_type=F32)


def build_first(w1):
    hidden = w1.shape[0]
    rows, cols = hidden * HR, 9 * KR
    i = iota((rows, 1), 0)
    channel, yi = lax.div(i, HR), lax.rem(i, HR)
    expand = onehot(channel == iota((rows, hidden), 1))
    by_row = dot(expand, w1).astype(BF16)
    j = iota((1, cols), 1)
    tap, r = lax.div(j, KR), lax.rem(j, KR)
    y = jnp.where(r < 40, r, r - KR)
    tap_offset = lax.div(tap, 3) * 9 + lax.rem(tap, 3)
    total = jnp.zeros((rows, cols), F32)
    for dy in range(3):
        pick = onehot(iota((27, cols), 0) == tap_offset + 3 * dy)
        total = total + jnp.where(y == yi + (dy - 2), dot(by_row, pick), 0.0)
    return total.astype(BF16)


def build_second(w2, first_row, last_row):
    hidden = w2.shape[0] // 2
    rows, cols = 192, hidden * HR
    i = iota((rows, 1), 0)
    group, y = lax.div(i, 32), lax.rem(i, 32)
    j = iota((1, cols), 1)
    yi = lax.rem(j, HR)
    inside = jnp.logical_not(((yi == 0) & first_row) | ((yi == HR - 1) & last_row))
    yi = jnp.where(inside, yi, -100)
    pick = onehot(lax.rem(iota((2 * hidden, cols), 0), hidden) == lax.div(j, HR))
    same = lax.rem(group, 2) == lax.div(iota((1, 2 * hidden), 1), hidden)
    blocks = []
    for dz in range(3):
        total = jnp.zeros((rows, cols), F32)
        for dy in range(3):
            select = onehot(iota((rows, 27), 1) == 9 * dz + 3 * dy + lax.div(group, 2))
            values = lax.dot_general(
                select, w2, (((1,), (1,)), ((), ())), preferred_element_type=F32
            )
            values = dot(jnp.where(same, values, 0.0).astype(BF16), pick)
            total = total + jnp.where(yi == y + dy, values, 0.0)
        blocks.append(total.astype(BF16))
    return blocks


def build_placing(owners_ref, slots, capacity):
    count = owners_ref.shape[0]
    target = [owners_ref[b] for b in range(count)]
    j = iota((1, 128), 1)
    brick = ((j & 31) >> 2) * 2 + (j >> 6)
    slot = jnp.zeros((1, 128), jnp.int32)
    for b in range(count):
        rank = jnp.int32(0)
        for other in range(b):
            rank = rank + jnp.where(target[other] == target[b], 1, 0)
        slot = jnp.where(brick == b, target[b] * capacity + rank, slot)
    column = slot * 8 + ((j >> 5) & 1) * 4 + (j & 3)
    i = iota((slots * 8, 1), 0)
    owner = lax.div(i, capacity * 8)
    row = (owner * capacity + lax.rem(i, capacity)) * 8 + lax.rem(lax.div(i, capacity), 8)
    return onehot(row == column)


def diffuse(carbon, oxygen, pore, organic, mass, lane):
    low, high = lane == 0, lane == BX - 1
    pore_c = [0.12 * v for v in pore]
    pore_o = [0.16 * v for v in pore]
    gain = [0.3 * v for v in organic]
    mass = [0.25 * v for v in mass]

    def laplace(field, q):
        z, y = q // 4, q % 4
        v = field[q]
        total = jnp.where(low, v, pltpu.roll(v, 1, 1)) + jnp.where(high, v, pltpu.roll(v, BX - 1, 1))
        near = 2
        for ok, at in ((z > 0, q - 4), (z < 3, q + 4), (y > 0, q - 1), (y < 3, q + 1)):
            if ok:
                total = total + field[at]
                near += 1
        return total - float(near) * v

    for _ in range(STEPS):
        carbon_new, oxygen_new = [], []
        for q in range(16):
            c, o = carbon[q], oxygen[q]
            uptake = mass[q] * c * o / ((0.5 + jnp.abs(c)) * (0.3 + jnp.abs(o)))
            carbon_new.append(c + pore_c[q] * laplace(carbon, q) + gain[q] - uptake)
            oxygen_new.append(o + pore_o[q] * laplace(oxygen, q) - uptake)
        carbon, oxygen = carbon_new, oxygen_new
    return carbon, oxygen


def kernel(
    sizes, capacity,
    density, w1_hbm, b1_hbm, w2_hbm, b2_hbm, owners_hbm,
    fractions, arrived,
    w1_ref, b1_ref, w2_ref, b2_ref, owners_ref, tile, first, second, shifted, hidden, frac, out,
    halo_send, halo_recv, brick_send, brick_recv, local_sem,
):
    n, n_gy, n_col = sizes
    slots = n * capacity
    here = (lax.axis_index("gz"), lax.axis_index("gy"), lax.axis_index("col"))
    me = here[0]

    def exists(offset):
        ok = None
        for position, size, o in zip(here, sizes, offset):
            test = None if o == 0 else (position + o >= 0) & (position + o < size)
            ok = test if ok is None else ok if test is None else ok & test
        return ok

    def device(offset):
        return {"gz": here[0] + offset[0], "gy": here[1] + offset[1], "col": here[2] + offset[2]}

    def halo(offset, index, receiver):
        seen = tuple(-o for o in offset) if not receiver else offset
        return pltpu.make_async_remote_copy(
            src_ref=region(density, (TAKE_Z, TAKE_Y, TAKE_X), seen),
            dst_ref=region(tile, (PLACE_Z, PLACE_Y, PLACE_X), seen),
            send_sem=halo_send.at[index],
            recv_sem=halo_recv.at[AROUND.index(seen)],
            device_id=device(offset),
            device_id_type=MESH,
        )

    small = [
        pltpu.make_async_copy(source, target, local_sem.at[4 + i])
        for i, (source, target) in enumerate(
            (
                (w1_hbm, w1_ref), (w2_hbm, w2_ref), (b1_hbm, b1_ref), (b2_hbm, b2_ref),
                (owners_hbm, owners_ref),
            )
        )
    ]
    for copy in small:
        copy.start()
    tile[...] = jnp.zeros_like(tile)
    barrier = pltpu.get_barrier_semaphore()
    expected = jnp.int32(n - 1)
    for offset in AROUND:
        ok = exists(offset)
        expected = expected + jnp.where(ok, 1, 0)

        @pl.when(ok)
        def _():
            pl.semaphore_signal(barrier, inc=1, device_id=device(offset), device_id_type=MESH)

    for j in range(1, n):
        pl.semaphore_signal(
            barrier, inc=1, device_id={"gz": lax.rem(me + j, n)}, device_id_type=MESH
        )
    own = pltpu.make_async_copy(
        density, region(tile, (PLACE_Z, PLACE_Y, PLACE_X), (0, 0, 0)), local_sem.at[0]
    )
    own.start()
    pl.semaphore_wait(barrier, expected)

    for index, offset in enumerate(AROUND):

        @pl.when(exists(offset))
        def _():
            halo(offset, index, False).start()

    for copy in small:
        copy.wait()
    first[...] = build_first(w1_ref[...])
    for dz, block in enumerate(build_second(w2_ref[...], here[1] == 0, here[1] == n_gy - 1)):
        second[dz] = block
    placing = build_placing(owners_ref, slots, capacity)
    channel = lax.div(iota((272, 1), 0), HR)
    bias1 = jnp.zeros((272, 1), F32)
    for o in range(8):
        bias1 = jnp.where(channel == o, b1_ref[o], bias1)
    bias2 = jnp.where(iota((64, 1), 0) < 32, b2_ref[0], b2_ref[1])
    lane = iota((1, BX), 1)
    keep = jnp.where(
        ((lane == 0) & (here[2] < n_col - 1)) | ((lane == BX - 1) & (here[2] > 0)), 1.0, 0.0
    )
    own.wait()
    for index, offset in enumerate(AROUND):

        @pl.when(exists(offset))
        def _():
            halo(offset, index, True).wait_recv()

    half_row = iota((16, 512), 0) < 8
    half_lane = iota((KR, BX), 1) < 64
    for zz in range(8):
        z = (zz + 6) % 8
        side = jnp.where(half_row, tile[z, 32:48, :].astype(F32), tile[z, 48:64, :].astype(F32))
        whole = jnp.concatenate([tile[z, 0:32, :].astype(F32), side], axis=0)
        edge = jnp.where(half_lane, whole[:, 256:384], whole[:, 384:512])
        whole = jnp.concatenate([whole[:, :256], edge], axis=1)
        base = zz * 3 * KR
        shifted[base : base + KR, :] = pltpu.roll(whole, 1, 1).astype(BF16)
        shifted[base + KR : base + 2 * KR, :] = whole.astype(BF16)
        shifted[base + 2 * KR : base + 3 * KR, :] = pltpu.roll(whole, LANES - 1, 1).astype(BF16)

    def hidden_slice(zi):
        value = dot(first[...], shifted[zi * 3 * KR : (zi + 3) * 3 * KR, :])
        value = jnp.maximum(value + bias1, 0.0)
        hidden[zi, :, 0:256] = value[:, :256].astype(BF16)
        hidden[zi, :, 256:384] = (value[:, 256:] * keep).astype(BF16)

    def brick_copy(j, z):
        to = lax.rem(me + j, n)
        return pltpu.make_async_remote_copy(
            src_ref=out.at[to, z],
            dst_ref=arrived.at[me, z],
            send_sem=brick_send.at[j, z],
            recv_sem=brick_recv.at[j, z],
            device_id={"gz": to},
            device_id_type=MESH,
        )

    hidden_slice(0)

    @pl.when(me == 0)
    def _():
        hidden[0] = jnp.zeros_like(hidden[0])

    hidden_slice(1)
    per = 8 * capacity
    for z in range(4):
        hidden_slice(z + 2)
        if z == 3:

            @pl.when(me == n - 1)
            def _():
                hidden[5] = jnp.zeros_like(hidden[5])

        total = jnp.zeros((192, LANES), F32)
        for dz in range(3):
            total = total + dot(second[dz], hidden[z + dz])
        value = (
            pltpu.roll(total[0:64], 1, 1) + total[64:128] + pltpu.roll(total[128:192], LANES - 1, 1)
        )[:, :256]
        value = (1.0 / (1.0 + jnp.exp(-(value + bias2)))).astype(BF16)
        frac[0, z] = value[:32]
        frac[1, z] = value[32:]
        placed = dot(placing, jnp.concatenate([value[:, :128], value[:, 128:]], axis=0)).astype(BF16)
        for d in range(n):
            out[d, z] = placed[d * per : (d + 1) * per]
        for j in range(1, n):
            brick_copy(j, z).start()
    store_frac = pltpu.make_async_copy(frac, fractions, local_sem.at[1])
    store_frac.start()
    keep_own = pltpu.make_async_copy(out.at[me], arrived.at[me], local_sem.at[2])
    keep_own.start()

    for j in range(1, n):
        source = lax.rem(me - j + n, n)
        for z in range(4):
            pltpu.make_async_remote_copy(
                src_ref=out.at[source, z],
                dst_ref=arrived.at[source, z],
                send_sem=brick_send.at[j, z],
                recv_sem=brick_recv.at[j, z],
                device_id={"gz": source},
                device_id_type=MESH,
            ).wait_recv()
    for index, offset in enumerate(AROUND):

        @pl.when(exists(offset))
        def _():
            halo(offset, index, False).wait_send()

    for j in range(1, n):
        for z in range(4):
            brick_copy(j, z).wait_send()
    store_frac.wait()
    keep_own.wait()


def diffusion_kernel(
    n, capacity,
    fractions_in, arrived_hbm, solutes, biomass,
    fractions, solutes_next,
    arrived, state, state_new, mass_in, mass, gathered,
    pass_sem, in_sem, out_sem,
):
    slots = n * capacity
    groups = slots // 8
    per_group = 8 // capacity
    through = pltpu.make_async_copy(fractions_in, fractions, pass_sem.at[0])

    def loads(g):
        span = pl.ds(g * per_group, per_group)
        return [
            pltpu.make_async_copy(source, target, in_sem.at[g, i])
            for i, (source, target) in enumerate(
                (
                    (arrived_hbm.at[span], arrived.at[span]),
                    (solutes.at[g], state.at[g]),
                    (biomass.at[g], mass_in.at[g]),
                )
            )
        ]

    for g in range(groups):
        for copy in loads(g):
            copy.start()
    through.start()

    def group_copy(g):
        return pltpu.make_async_copy(state_new.at[g], solutes_next.at[g], out_sem.at[g])

    for g in range(groups):
        for copy in loads(g):
            copy.wait()
        mass[...] = mass_in[g].astype(F32)
        values = [[None] * 16, [None] * 16]
        if capacity == 8:
            for z in range(4):
                for o in range(2):
                    for pair in range(2):
                        at = o * 32 + pair * 16
                        both = arrived[g, z, at : at + 16, :].astype(F32)
                        values[o][z * 4 + pair * 2] = both[:8]
                        values[o][z * 4 + pair * 2 + 1] = both[8:]
        else:
            for part in range(per_group):
                for z in range(4):
                    block = arrived[g * per_group + part, z].astype(F32)
                    for row in range(8):
                        q = row // 4 * 16 + z * 4 + row % 4
                        gathered[q, part * capacity : (part + 1) * capacity, :] = block[
                            row * capacity : (row + 1) * capacity
                        ]
            values = [[gathered[o * 16 + q] for q in range(16)] for o in range(2)]
        carbon = [state[g, pl.ds(q, 8, stride=32), :] for q in range(16)]
        oxygen = [state[g, pl.ds(16 + q, 8, stride=32), :] for q in range(16)]
        held = [mass[pl.ds(q, 8, stride=16), :] for q in range(16)]
        carbon, oxygen = diffuse(carbon, oxygen, *values, held, iota((8, BX), 1))
        for q in range(16):
            state_new[g, pl.ds(q, 8, stride=32), :] = carbon[q]
            state_new[g, pl.ds(16 + q, 8, stride=32), :] = oxygen[q]
        group_copy(g).start()
    for g in range(groups):
        group_copy(g).wait()
    through.wait()


def per_device(
    sizes, density, first_kernel, first_bias, second_kernel, second_bias, owners, solutes, biomass
):
    n = sizes[0]
    slots = solutes.shape[3]
    capacity = slots // n
    per = 8 * capacity
    anywhere = pl.BlockSpec(memory_space=pltpu.HBM)
    groups = slots // 8
    fractions, arrived = pl.pallas_call(
        functools.partial(kernel, sizes, capacity),
        out_shape=(
            jax.ShapeDtypeStruct((2,) + density.shape, BF16),
            jax.ShapeDtypeStruct((n, 4, per, BX), BF16),
        ),
        in_specs=[anywhere] * 6,
        out_specs=(anywhere, anywhere),
        scratch_shapes=[
            pltpu.VMEM((8, 27), BF16),
            pltpu.SMEM((8,), F32),
            pltpu.VMEM((16, 27), BF16),
            pltpu.SMEM((2,), F32),
            pltpu.SMEM((16,), jnp.int32),
            pltpu.VMEM((8, 64, 512), BF16),
            pltpu.VMEM((272, 9 * KR), BF16),
            pltpu.VMEM((3, 192, 272), BF16),
            pltpu.VMEM((8 * 3 * KR, LANES), BF16),
            pltpu.VMEM((6, 272, LANES), BF16),
            pltpu.VMEM((2,) + density.shape, BF16),
            pltpu.VMEM((n, 4, per, BX), BF16),
            pltpu.SemaphoreType.DMA((26,)),
            pltpu.SemaphoreType.DMA((26,)),
            pltpu.SemaphoreType.DMA((n, 4)),
            pltpu.SemaphoreType.DMA((n, 4)),
            pltpu.SemaphoreType.DMA((9,)),
        ],
        compiler_params=pltpu.CompilerParams(
            collective_id=0, has_side_effects=True, vmem_limit_bytes=64 * 1024 * 1024
        ),
    )(
        density,
        first_kernel.transpose(2, 1, 0).reshape(8, 27),
        first_bias,
        second_kernel.transpose(1, 2, 0).reshape(16, 27),
        second_bias,
        owners.reshape(-1),
    )
    fractions, solutes_next = pl.pallas_call(
        functools.partial(diffusion_kernel, n, capacity),
        out_shape=(
            jax.ShapeDtypeStruct((2,) + density.shape, BF16),
            jax.ShapeDtypeStruct((groups, 256, BX), F32),
        ),
        in_specs=[anywhere] * 4,
        out_specs=(anywhere, anywhere),
        scratch_shapes=[
            pltpu.VMEM((n, 4, per, BX), BF16),
            pltpu.VMEM((groups, 256, BX), F32),
            pltpu.VMEM((groups, 256, BX), F32),
            pltpu.VMEM((groups, 128, BX), BF16),
            pltpu.VMEM((128, BX), F32),
            pltpu.VMEM((32, 8, BX), F32),
            pltpu.SemaphoreType.DMA((1,)),
            pltpu.SemaphoreType.DMA((groups, 3)),
            pltpu.SemaphoreType.DMA((groups,)),
        ],
        compiler_params=pltpu.CompilerParams(vmem_limit_bytes=64 * 1024 * 1024),
    )(
        fractions,
        arrived,
        solutes.reshape(groups, 256, BX),
        biomass.reshape(groups, 128, BX),
    )
    return fractions, solutes_next.reshape(solutes.shape)


def solution(mesh):
    sizes = tuple(mesh.shape[axis] for axis in ("gz", "gy", "col"))
    return jax.shard_map(
        functools.partial(per_device, sizes),
        mesh=mesh,
        in_specs=(
            P(("cores", "gz"), "gy", "col"),
            P(),
            P(),
            P(),
            P(),
            P(("cores", "gz"), "gy", "col", None, None),
            P(("cores", "gz"), "gy", "col", None, None, None, None, None),
            P(("cores", "gz"), "gy", "col", None, None, None, None),
        ),
        out_specs=(
            P(None, ("cores", "gz"), "gy", "col"),
            P(("cores", "gz"), "gy", "col", None, None, None, None, None),
        ),
        check_vma=False,
    )
```
